32 devices in a mesh: wide: 8 (over z, y), narrow: 4 (over x, core).
Axes of the slice: x: 2, y: 2, z: 4, core: 2. Of those that a mesh axis runs over, the one named last changes fastest.
Arguments:
- inputs: bfloat16 [2, 1024, 16, 512], P(None, 'narrow', 'wide')
- cotangent: bfloat16 [2, 1024, 16, 512], P(None, 'narrow', 'wide'), may hold values from -6 to 6
- lengths: int32 [2, 16], P(None, 'wide'), may hold values from 102 to 1024, as said below
- ffn1_in: bfloat16 [512, 2048], P('wide', 'narrow'), may hold values from -0.25 to 0.25
- ffn1_out: bfloat16 [2048, 512], P('narrow', 'wide'), may hold values from -0.25 to 0.25
- attn_in: bfloat16 [512, 3, 512], P('wide', None, 'narrow'), may hold values from -0.25 to 0.25
- pos_proj: bfloat16 [512, 512], P('wide', 'narrow'), may hold values from -0.25 to 0.25
- attn_out: bfloat16 [512, 512], P('narrow', 'wide'), may hold values from -1.5 to 1.5
- conv_in: bfloat16 [512, 2, 512], P('wide', None, 'narrow'), may hold values from -0.25 to 0.25
- depthwise: bfloat16 [32, 512], P('wide', 'narrow'), may hold values from -1 to 1
- conv_out: bfloat16 [512, 512], P('narrow', 'wide'), may hold values from -0.375 to 0.375
- ffn2_in: bfloat16 [512, 2048], P('wide', 'narrow'), may hold values from -0.25 to 0.25
- ffn2_out: bfloat16 [2048, 512], P('narrow', 'wide'), may hold values from -0.25 to 0.25
- row_gains: bfloat16 [5, 512], replicated, may hold values from 0.099609375 to 1.8984375
- row_biases: bfloat16 [9, 512], replicated, may hold values from -2 to 2
- unit_biases: bfloat16 [5, 512], P(None, 'narrow'), may hold values from -3 to 3
- ffn_biases: bfloat16 [2, 2048], P(None, 'narrow'), may hold values from -3 to 3
- norm_affine: bfloat16 [2, 512], P(None, 'narrow'), may hold values from 0.099609375 to 1.8984375
Outputs:
- layer_out: bfloat16 [2, 1024, 16, 512], P(None, 'narrow', 'wide')
- input_grad: float32 [2, 1024, 16, 512], P(None, 'narrow', 'wide')
- grad_ffn1_in: float32 [512, 2048], P('wide', 'narrow')
- grad_ffn1_out: float32 [2048, 512], P('narrow', 'wide')
- grad_attn_in: float32 [512, 3, 512], P('wide', None, 'narrow')
- grad_pos_proj: float32 [512, 512], P('wide', 'narrow')
- grad_attn_out: float32 [512, 512], P('narrow', 'wide')
- grad_conv_in: float32 [512, 2, 512], P('wide', None, 'narrow')
- grad_depthwise: float32 [32, 512], P('wide', 'narrow')
- grad_conv_out: float32 [512, 512], P('narrow', 'wide')
- grad_ffn2_in: float32 [512, 2048], P('wide', 'narrow')
- grad_ffn2_out: float32 [2048, 512], P('narrow', 'wide')
- grad_row_gains: float32 [5, 512], replicated
- grad_row_biases: float32 [9, 512], replicated
- grad_unit_biases: float32 [5, 512], P(None, 'narrow')
- grad_ffn_biases: float32 [2, 2048], P(None, 'narrow')
- grad_norm_affine: float32 [2, 512], P(None, 'narrow')
The draws below stay inside these ranges and needn't reach their ends.
Inputs may be any that keep to these rules, and one draw needn't show every extreme that they name: `lengths`: in each micro-batch one utterance has 1024 frames and another has the fewest frames allowed.
All inputs are finite; a program needn't handle non-finite values.
Results may differ from the reference program's by a relative error of at most 0.03.
Values may be sent and summed in bfloat16 or wider, within the bound.
No kernel may reach another device: no remote copies, remote signals or barrier semaphores. Data moves between devices by JAX's collectives and lax.ppermute only.
A program may use at most 320 MiB of HBM per device.

```python
import math
import jax
import jax.numpy as jnp
from jax import lax

D = 512
HEADS = 8
FF = 2048
KERNEL = 32
HEAD_DIM = 64
LMAX = 1024
MB = 2
UTTS = 16


def draw_inputs(key, part):
    base_key = jax.random.fold_in(key, 11)
    offset_key = jax.random.fold_in(key, 12)
    shape_all = (MB, LMAX, UTTS, D)
    base = jax.random.normal(base_key, shape_all, jnp.float32)
    offsets = jax.random.normal(offset_key, (UTTS, D), jnp.float32)
    ramp = 0.5 + 1.5 * jnp.arange(UTTS).astype(jnp.float32) / (UTTS - 1)
    values = base + ramp[None, None, :, None] * offsets[None, None, :, :]
    return values.astype(jnp.bfloat16)


def draw_lengths(key, part):
    shortest = max(1, LMAX // 10)
    values = jax.random.randint(jax.random.fold_in(key, 21), (MB, UTTS), shortest, LMAX + 1)

    def one_order(sub_key):
        return jax.random.permutation(sub_key, UTTS)
    orders = jax.vmap(one_order)(jax.random.split(jax.random.fold_in(key, 22), MB))
    slots = jnp.arange(UTTS)[None, :]
    values = jnp.where(slots == orders[:, 0:1], LMAX, values)
    values = jnp.where(slots == orders[:, 1:2], shortest, values)
    return values.astype(jnp.int32)


def spiked(values, key, source, target, blocks, factor):
    def block_of(axis_at):
        return (jnp.arange(values.shape[axis_at]) // (values.shape[axis_at] // blocks)).reshape((-1,) + (1,) * (values.ndim - 1 - axis_at))

    first = jax.random.permutation(key, blocks)[block_of(target)]
    second = (block_of(target) + blocks // 2) % blocks
    return jnp.where((block_of(source) == first) | (block_of(source) == second), factor * values, values)


def levels(key, shape, pieces, low, high):
    gain = 1.0
    for axis_at, shards_of in pieces:
        heights = jax.random.uniform(jax.random.fold_in(jax.random.fold_in(key, 6), axis_at), (shards_of,), jnp.float32, low / len(pieces), high / len(pieces))
        gain = gain * jnp.repeat(jnp.exp(heights), shape[axis_at] // shards_of).reshape((-1,) + (1,) * (len(shape) - 1 - axis_at))
    return gain


def bell_draw(stream_key, shape, deviation, reach, cuts=(), held_as=jnp.bfloat16):
    values = deviation * jax.random.normal(stream_key, shape, jnp.float32)
    if cuts:
        values = values * levels(stream_key, shape, cuts, -0.22, 0.18)
    return jnp.clip(values, -reach, reach).astype(held_as)


def noise_with(key, shape, scale, reach, cuts, heavy, dtype=jnp.bfloat16):
    array = scale * jax.random.normal(key, shape, jnp.float32)
    if cuts:
        array = array * levels(key, shape, cuts, -0.22, 0.18)
    return jnp.clip(spiked(array, jax.random.fold_in(key, 3), *heavy), -reach, reach).astype(dtype)


def setup_inputs(seed: int = 0) -> dict:
    key_of = jax.random.split(jax.random.key(seed), 19)
    return {
        "inputs": draw_inputs(jax.random.fold_in(key_of[18], 71), 0),
        "cotangent": noise_with(key_of[1], (MB, LMAX, UTTS, D), 1.0, 6.0, ((1, 4), (2, 8)), (2, 3, 8, 2.0)),
        "lengths": draw_lengths(jax.random.fold_in(key_of[18], 71), 0),
        "ffn1_in": bell_draw(key_of[3], (D, FF), D ** -0.5, 0.25, ((0, 8), (1, 4))),
        "ffn1_out": bell_draw(key_of[4], (FF, D), (FF // 4) ** -0.5, 0.25, ((0, 4), (1, 8))),
        "attn_in": bell_draw(key_of[5], (D, 3, D), D ** -0.5, 0.25, ((0, 8), (2, 4))),
        "pos_proj": bell_draw(key_of[6], (D, D), D ** -0.5, 0.25, ((0, 8), (1, 4))),
        "attn_out": bell_draw(key_of[7], (D, D), (D // 32) ** -0.5, 1.5, ((0, 4), (1, 8))),
        "conv_in": bell_draw(key_of[8], (D, 2, D), D ** -0.5, 0.25, ((0, 8), (2, 4))),
        "depthwise": bell_draw(key_of[9], (KERNEL, D), KERNEL ** -0.5, 1.0, ((0, 8), (1, 4))),
        "conv_out": bell_draw(key_of[10], (D, D), (D // 2) ** -0.5, 0.375, ((0, 4), (1, 8))),
        "ffn2_in": bell_draw(key_of[11], (D, FF), D ** -0.5, 0.25, ((0, 8), (1, 4))),
        "ffn2_out": bell_draw(key_of[12], (FF, D), (FF // 4) ** -0.5, 0.25, ((0, 4), (1, 8))),
        "row_gains": jnp.clip(1.0 + 0.18 * jax.random.normal(key_of[13], (5, D), jnp.float32), 0.099609375, 1.8984375).astype(jnp.bfloat16),
        "row_biases": bell_draw(key_of[14], (9, D), 0.3, 2.0),
        "unit_biases": bell_draw(key_of[15], (5, D), 0.5, 3.0, ((1, 4),)),
        "ffn_biases": bell_draw(key_of[16], (2, FF), 0.5, 3.0, ((1, 4),)),
        "norm_affine": jnp.clip(1.0 + 0.18 * jax.random.normal(key_of[17], (2, D), jnp.float32), 0.099609375, 1.8984375).astype(jnp.bfloat16),
    }


@jax.custom_vjp
def low(v):
    return lax.optimization_barrier(v.astype(jnp.bfloat16)).astype(jnp.float32)

@jax.custom_vjp
def low_back(v):
    return v

def low_keep(v):
    return (low(v), None)

def low_pass(kept, grad):
    return (grad,)

def back_keep(v):
    return (v, None)

def back_low(kept, grad):
    return (low(grad),)
low.defvjp(low_keep, low_pass)
low_back.defvjp(back_keep, back_low)
HIGHEST = lax.Precision.HIGHEST
EPSILON = 1e-05
MASKED = -1e+30

def layer_norm(values_in, scale_row, shift_row):
    center = values_in - lax.optimization_barrier(jnp.mean(values_in, axis=-1, keepdims=True))
    spread = lax.optimization_barrier(jnp.mean(center * center, axis=-1, keepdims=True))
    return center * lax.rsqrt(spread + EPSILON) * scale_row + shift_row

def position_table(length, feature_count):
    offsets = (length - 1 - jnp.arange(2 * length - 1)).astype(jnp.float32)
    freq_index = jnp.arange(feature_count // 2).astype(jnp.float32)
    frequency = jnp.exp(freq_index * (-2.0 * math.log(10000.0) / feature_count))
    angles = offsets[:, None] * frequency[None, :]
    return jnp.stack([jnp.sin(angles), jnp.cos(angles)], axis=-1).reshape(2 * length - 1, feature_count)

def relative(raw_scores, block_rows, key_count):
    padded = jnp.pad(raw_scores, ((0, 0), (0, 1)))
    flattened = padded.reshape(-1)
    flattened = lax.slice_in_dim(flattened, block_rows - 1, block_rows - 1 + block_rows * (block_rows + key_count - 1))
    return flattened.reshape(block_rows, block_rows + key_count - 1)[:, :key_count]

def attend_head(query_c, query_p, key_head, value_head, pos_head, valid_keys):
    length = key_head.shape[0]
    scale = 1.0 / math.sqrt(HEAD_DIM)
    content = jnp.dot(query_c, key_head.T, precision=HIGHEST)
    raw_scores = jnp.dot(query_p, pos_head.T, precision=HIGHEST)
    scores = low_back((content + relative(raw_scores, length, length)) * scale)
    scores = jnp.where(valid_keys[None, :], scores, MASKED)
    attention_probs = low(jax.nn.softmax(scores, axis=-1))
    return jnp.dot(attention_probs, value_head, precision=HIGHEST)

def feed_forward(stream, scale_row, shift_row, w_in, hidden_bias, w_out, out_bias):
    normed = low(layer_norm(stream, scale_row, shift_row))
    pre_act = low_back(jnp.einsum('lud,df->luf', normed, w_in, precision=HIGHEST) + hidden_bias)
    activated = low(jax.nn.silu(pre_act))
    result = low_back(jnp.einsum('luf,fd->lud', activated, w_out, precision=HIGHEST))
    return stream + 0.5 * (result + out_bias)

def attention_block(stream, scale_row, shift_row, w_qkv, w_pos, w_out, out_bias, unit_rows, valid):
    length, utter_count, feature_count = stream.shape
    normed = low(layer_norm(stream, scale_row, shift_row))
    project = jnp.einsum('lud,dke->luke', normed, w_qkv, precision=HIGHEST)
    query = low_back(project[:, :, 0])
    key_all = low(low_back(project[:, :, 1]))
    value_all = low(low_back(project[:, :, 2] + unit_rows[0]))
    query_c = low(query + unit_rows[1])
    query_p = low(query + unit_rows[2])
    pos_table = low(position_table(length, feature_count))
    pos_all = low(low_back(jnp.dot(pos_table, w_pos, precision=HIGHEST)))
    pos_heads = pos_all.reshape(2 * length - 1, HEADS, HEAD_DIM)

    def to_heads(values_in):
        return jnp.moveaxis(values_in.reshape(length, utter_count, HEADS, HEAD_DIM), 1, 0)

    def one_utterance(packed):
        per_head = jax.vmap(attend_head, in_axes=(1, 1, 1, 1, 1, None), out_axes=1)
        return per_head(packed[0], packed[1], packed[2], packed[3], pos_heads, packed[4])
    context = lax.map(jax.checkpoint(one_utterance), (to_heads(query_c), to_heads(query_p), to_heads(key_all), to_heads(value_all), valid.T))
    context = jnp.moveaxis(context, 0, 1).reshape(length, utter_count, feature_count)
    context = low(low_back(context))
    result = low_back(jnp.einsum('lue,ed->lud', context, w_out, precision=HIGHEST))
    return stream + result + out_bias

def conv_block(stream, scale_row, shift_row, w_in, unit_rows, w_depth, affine, w_out, out_bias, mask_full, count):
    length = stream.shape[0]
    normed = low(layer_norm(stream, scale_row, shift_row))
    pre_act = low_back(jnp.einsum('lud,dke->luke', normed, w_in, precision=HIGHEST) + unit_rows[3:5])
    gated = pre_act[:, :, 0] * jax.nn.sigmoid(pre_act[:, :, 1]) * mask_full[:, :, None]
    tap_count = w_depth.shape[0]
    padded = jnp.pad(gated, ((tap_count // 2 - 1, tap_count // 2), (0, 0), (0, 0)))
    mixed = w_depth[0] * padded[0:length]
    for tap_index in range(1, tap_count):
        mixed = mixed + w_depth[tap_index] * padded[tap_index:tap_index + length]
    masked = mixed * mask_full[:, :, None]
    mean_row = lax.optimization_barrier(jnp.sum(masked, axis=(0, 1))) / count
    center = mixed - mean_row
    spread = lax.optimization_barrier(jnp.sum(center * center * mask_full[:, :, None], axis=(0, 1))) / count
    normal = center * lax.rsqrt(spread + EPSILON) * affine[0] + affine[1]
    activated = low(jax.nn.silu(normal))
    result = low_back(jnp.einsum('lue,ed->lud', activated, w_out, precision=HIGHEST))
    return stream + result + out_bias

def forward(stream, params, valid, mask_full, count):
    ffn1_in, ffn1_out, attn_in, pos_proj, attn_out, conv_in, depthwise, conv_out, ffn2_in, ffn2_out, row_gains, row_biases, unit_biases, ffn_biases, norm_affine = params
    stream = feed_forward(stream, row_gains[0], row_biases[0], ffn1_in, ffn_biases[0], ffn1_out, row_biases[5])
    stream = attention_block(stream, row_gains[1], row_biases[1], attn_in, pos_proj, attn_out, row_biases[6], unit_biases, valid)
    stream = conv_block(stream, row_gains[2], row_biases[2], conv_in, unit_biases, depthwise, norm_affine, conv_out, row_biases[7], mask_full, count)
    stream = feed_forward(stream, row_gains[3], row_biases[3], ffn2_in, ffn_biases[1], ffn2_out, row_biases[8])
    return layer_norm(stream, row_gains[4], row_biases[4])

def reference(inputs, cotangent, lengths, ffn1_in, ffn1_out, attn_in, pos_proj, attn_out, conv_in, depthwise, conv_out, ffn2_in, ffn2_out, row_gains, row_biases, unit_biases, ffn_biases, norm_affine):
    params = tuple((item.astype(jnp.float32) for item in (ffn1_in, ffn1_out, attn_in, pos_proj, attn_out, conv_in, depthwise, conv_out, ffn2_in, ffn2_out, row_gains, row_biases, unit_biases, ffn_biases, norm_affine)))
    outputs = []
    input_grads = []
    totals = None
    for micro_index in range(MB):
        valid = jnp.arange(LMAX)[:, None] < lengths[micro_index][None, :]
        mask_full = valid.astype(jnp.float32)
        count = jnp.sum(lengths[micro_index]).astype(jnp.float32)

        def run_layer(stream, *weights_in):
            return forward(stream, weights_in, valid, mask_full, count)
        result, pull = jax.vjp(run_layer, inputs[micro_index].astype(jnp.float32), *params)
        grads = pull(cotangent[micro_index].astype(jnp.float32) * mask_full[:, :, None])
        outputs.append(result.astype(jnp.bfloat16))
        input_grads.append(grads[0])
        if totals is None:
            totals = grads[1:]
        else:
            totals = tuple((first + second for first, second in zip(totals, grads[1:])))
    return (jnp.stack(outputs), jnp.stack(input_grads), totals[0], totals[1], totals[2], totals[3], totals[4], totals[5], totals[6], totals[7], totals[8], totals[9], totals[10], totals[11], totals[12], totals[13], totals[14])
```

```python
from functools import partial
import math

import jax
import jax.numpy as jnp
import numpy as np
from jax import lax
from jax.experimental import pallas as pl
from jax.experimental.pallas import tpu as pltpu
from jax.sharding import PartitionSpec as P

HEAD_DIM = 64
EPSILON = 1e-05
MASKED = -1e30
LANES = 128
ROWS = 256
CONV_ROWS = 128
SMALL_ROWS = 15
BF = jnp.bfloat16
F32 = jnp.float32
NN = (((1,), (0,)), ((), ()))
NT = (((1,), (1,)), ((), ()))


def dot(left, right, dims=NN):
    return lax.dot_general(left, right, dims, preferred_element_type=F32)


def sigmoid(values):
    return 0.5 * jnp.tanh(0.5 * values) + 0.5


def normal_rows(values):
    center = values - jnp.mean(values, axis=-1, keepdims=True)
    inverse = lax.rsqrt(jnp.mean(center * center, axis=-1, keepdims=True) + EPSILON)
    return center * inverse, inverse


def normal_rows_back(upstream, normal, inverse, gain):
    scaled = upstream * gain
    plain = jnp.mean(scaled, axis=-1, keepdims=True)
    cross = jnp.mean(scaled * normal, axis=-1, keepdims=True)
    return inverse * (scaled - plain - normal * cross)


def column_sum(values):
    return jnp.sum(values, axis=0, keepdims=True)


def chunk(index, rows=ROWS):
    return pl.ds(pl.multiple_of(index * rows, rows), rows)


def first_step(axis_step):
    return pl.when(axis_step == 0)


def full(shape):
    return pl.BlockSpec(shape, lambda *_: (0,) * len(shape), pipeline_mode=pl.Buffered(1))


def params(**more):
    return pltpu.CompilerParams(vmem_limit_bytes=62 * 1024 * 1024, **more)


def ffn_forward_kernel(x_ref, gain_ref, bias_ref, w_ref, hidden_ref, out_ref, a_ref, h_ref):
    step = pl.program_id(0)
    count = x_ref.shape[0] // ROWS
    width = a_ref.shape[1]

    @pl.when(step == 0)
    def _():
        @pl.loop(0, count)
        def _(i):
            rows = chunk(i)
            normal, _ = normal_rows(x_ref[rows, :].astype(F32))
            h_ref[rows, :] = (normal * gain_ref[0:1, :] + bias_ref[0:1, :]).astype(BF)
            out_ref[rows, :] = jnp.zeros((ROWS, out_ref.shape[1]), F32)

    @pl.loop(0, count)
    def _(i):
        rows = chunk(i)
        pre = dot(h_ref[rows, :], w_ref[:, :width]) + hidden_ref[0:1, :]
        a_ref[rows, :] = pre.astype(BF)
        act = (pre * sigmoid(pre)).astype(BF)
        out_ref[rows, :] += dot(act, w_ref[:, width:], NT)

    @pl.when(step == pl.num_programs(0) - 1)
    def _():
        @pl.loop(0, count)
        def _(i):
            rows = chunk(i)
            out_ref[rows, :] = x_ref[rows, :].astype(F32) + 0.5 * (
                out_ref[rows, :] + bias_ref[5:6, :]
            )


def ffn_forward(x, gains, biases, weights, hidden):
    length, features = x.shape
    blocks = weights.shape[0] // features
    width = hidden.shape[1] // blocks
    return pl.pallas_call(
        ffn_forward_kernel,
        name="ffn_forward",
        grid=(blocks,),
        in_specs=[
            full(x.shape),
            full(gains.shape),
            full(biases.shape),
            pl.BlockSpec((features, 2 * width), lambda n: (n, 0)),
            pl.BlockSpec((2, width), lambda n: (0, n)),
        ],
        out_specs=[
            full((length, features)),
            pl.BlockSpec((length, width), lambda n: (0, n)),
        ],
        out_shape=[
            jax.ShapeDtypeStruct((length, features), F32),
            jax.ShapeDtypeStruct((length, blocks * width), BF),
        ],
        scratch_shapes=[pltpu.VMEM((length, features), BF)],
        compiler_params=params(),
    )(x, gains, biases, weights, hidden)


def ffn_backward_kernel(
    up_ref, x_ref, gain_ref, bias_ref, w_ref, a_ref,
    out_ref, grad_ref, hidden_grad_ref, vec_ref,
    ht_ref, df_ref, dft_ref, s_ref, da_ref,
):
    step = pl.program_id(0)
    length, features = x_ref.shape
    count = length // ROWS
    width = a_ref.shape[1]

    @pl.when(step == 0)
    def _():
        vec_ref[...] = jnp.zeros(vec_ref.shape, F32)

        @pl.loop(0, count)
        def _(i):
            rows = chunk(i)
            normal, _ = normal_rows(x_ref[rows, :].astype(F32))
            hidden = normal * gain_ref[0:1, :] + bias_ref[0:1, :]
            ht_ref[:, rows] = hidden.T.astype(BF)
            half = 0.5 * up_ref[rows, :]
            df_ref[rows, :] = half.astype(BF)
            dft_ref[:, rows] = half.T.astype(BF)
            vec_ref[2:3, :] += column_sum(half)
            out_ref[rows, :] = jnp.zeros((ROWS, features), F32)

    hidden_grad_ref[...] = jnp.zeros(hidden_grad_ref.shape, F32)

    @pl.loop(0, count)
    def _(i):
        rows = chunk(i)
        pre = a_ref[rows, :].astype(F32)
        sigma = sigmoid(pre)
        s_ref[rows, :] = (pre * sigma).astype(BF)
        grad_act = dot(df_ref[rows, :], w_ref[:, width:])
        grad_pre = (grad_act * (sigma * (1.0 + pre * (1.0 - sigma)))).astype(BF)
        da_ref[rows, :] = grad_pre
        hidden_grad_ref[...] += column_sum(grad_pre.astype(F32))
        out_ref[rows, :] += dot(grad_pre, w_ref[:, :width], NT)

    @pl.loop(0, features // LANES)
    def _(i):
        rows = chunk(i, LANES)
        grad_ref[rows, :width] = dot(ht_ref[rows, :], da_ref[...]).astype(BF)
        grad_ref[rows, width:] = dot(dft_ref[rows, :], s_ref[...]).astype(BF)

    @pl.when(step == pl.num_programs(0) - 1)
    def _():
        @pl.loop(0, count)
        def _(i):
            rows = chunk(i)
            grad_normed = out_ref[rows, :]
            normal, inverse = normal_rows(x_ref[rows, :].astype(F32))
            vec_ref[0:1, :] += column_sum(grad_normed * normal)
            vec_ref[1:2, :] += column_sum(grad_normed)
            out_ref[rows, :] = up_ref[rows, :] + normal_rows_back(
                grad_normed, normal, inverse, gain_ref[0:1, :]
            )


def ffn_backward(upstream, x, gains, biases, weights, a_saved, grads):
    length, features = x.shape
    blocks = weights.shape[0] // features
    width = a_saved.shape[1] // blocks

    def kernel(up, xr, g, b, w, a, grads_in, *rest):
        ffn_backward_kernel(up, xr, g, b, w, a, *rest)

    return pl.pallas_call(
        kernel,
        name="ffn_backward",
        grid=(blocks,),
        in_specs=[
            full(upstream.shape),
            full(x.shape),
            full(gains.shape),
            full(biases.shape),
            pl.BlockSpec((features, 2 * width), lambda n: (n, 0)),
            pl.BlockSpec((length, width), lambda n: (0, n)),
            pl.BlockSpec(memory_space=pl.ANY),
        ],
        out_specs=[
            full((length, features)),
            pl.BlockSpec((features, 2 * width), lambda n: (n, 0)),
            pl.BlockSpec((1, width), lambda n: (0, n)),
            full((8, features)),
        ],
        out_shape=[
            jax.ShapeDtypeStruct((length, features), F32),
            jax.ShapeDtypeStruct(grads.shape, BF),
            jax.ShapeDtypeStruct((1, blocks * width), F32),
            jax.ShapeDtypeStruct((8, features), F32),
        ],
        scratch_shapes=[
            pltpu.VMEM((features, length), BF),
            pltpu.VMEM((length, features), BF),
            pltpu.VMEM((features, length), BF),
            pltpu.VMEM((length, width), BF),
            pltpu.VMEM((length, width), BF),
        ],
        input_output_aliases={6: 1},
        compiler_params=params(),
    )(upstream, x, gains, biases, weights, a_saved, grads)


def attention_forward_kernel(
    x_ref, gain_ref, bias_ref, w_ref, unit_ref, table_ref, masked_ref,
    out_ref, h_ref, qc_ref, qp_ref, k_ref, v_ref, pos_ref, ctx_ref, p_ref,
):
    step = pl.program_id(0)
    length, features = x_ref.shape
    count = length // ROWS
    window = length + ROWS
    scale = 1.0 / math.sqrt(HEAD_DIM)

    @pl.when(step == 0)
    def _():
        @pl.loop(0, count)
        def _(i):
            rows = chunk(i)
            values = x_ref[rows, :]
            normal, _ = normal_rows(values)
            h_ref[rows, :] = (normal * gain_ref[1:2, :] + bias_ref[1:2, :]).astype(BF)
            out_ref[rows, :] = values + bias_ref[6:7, :]

    @pl.loop(0, count)
    def _(i):
        rows = chunk(i)
        project = dot(h_ref[rows, :], w_ref[:, : 3 * LANES])
        query = project[:, :LANES]
        qc_ref[rows, :] = ((query + unit_ref[1:2, :]).astype(BF) * scale).astype(BF)
        qp_ref[rows, :] = ((query + unit_ref[2:3, :]).astype(BF) * scale).astype(BF)
        k_ref[rows, :] = project[:, LANES : 2 * LANES].astype(BF)
        v_ref[rows, :] = (project[:, 2 * LANES :] + unit_ref[0:1, :]).astype(BF)

    @pl.loop(0, 2 * count)
    def _(i):
        rows = chunk(i)
        pos_ref[rows, :] = dot(table_ref[rows, :], w_ref[:, 3 * LANES : 4 * LANES]).astype(BF)

    lane = lax.broadcasted_iota(jnp.int32, (ROWS, LANES), 1) < HEAD_DIM

    @pl.loop(0, count)
    def _(i):
        rows = chunk(i)
        begin = pl.multiple_of((length - ROWS) - i * ROWS, ROWS)
        positions = pos_ref[pl.ds(begin, window), :]
        results = []
        for head in range(2):
            own = lane if head == 0 else jnp.logical_not(lane)
            rows_c = jnp.where(own, qc_ref[rows, :], jnp.zeros((), BF))
            rows_p = jnp.where(own, qp_ref[rows, :], jnp.zeros((), BF))
            raw = dot(rows_p, positions, NT)
            shifted = pltpu.roll(raw, length + 1, 1, stride=1, stride_axis=0)[:, :length]
            scores = dot(rows_c, k_ref[...], NT) + shifted + masked_ref[...]
            top = jnp.max(scores, axis=1, keepdims=True)
            powers = jnp.exp(scores - top)
            inverse = 1.0 / jnp.sum(powers, axis=1, keepdims=True)
            probs = (powers * inverse).astype(BF)
            p_ref[head, rows, :] = probs
            results.append(dot(probs, v_ref[...]))
        context = jnp.where(lane, results[0], results[1])
        ctx_ref[rows, :] = context
        out_ref[rows, :] += dot(context.astype(BF), w_ref[:, 4 * LANES :], NT)


def attention_forward(x, gains, biases, weights, units, table, masked):
    length, features = x.shape
    blocks = weights.shape[0] // features
    column = pl.BlockSpec((length, LANES), lambda n: (0, n))
    low = jax.ShapeDtypeStruct((length, features), BF)
    return pl.pallas_call(
        attention_forward_kernel,
        name="attention_forward",
        grid=(blocks,),
        in_specs=[
            full(x.shape),
            full(gains.shape),
            full(biases.shape),
            pl.BlockSpec((features, 5 * LANES), lambda n: (n, 4)),
            pl.BlockSpec((5, LANES), lambda n: (0, n)),
            full(table.shape),
            full(masked.shape),
        ],
        out_specs=[
            full((length, features)),
            full((length, features)),
            column,
            column,
            column,
            column,
            pl.BlockSpec((2 * length, LANES), lambda n: (0, n)),
            column,
            pl.BlockSpec((2, length, length), lambda n: (n, 0, 0)),
        ],
        out_shape=[
            jax.ShapeDtypeStruct((length, features), F32),
            low,
            low,
            low,
            low,
            low,
            jax.ShapeDtypeStruct((2 * length, features), BF),
            jax.ShapeDtypeStruct((length, features), F32),
            jax.ShapeDtypeStruct((2 * blocks, length, length), BF),
        ],
        compiler_params=params(),
    )(x, gains, biases, weights, units, table, masked)


def attention_backward_kernel(
    up_ref, x_ref, h_ref, gain_ref, w_ref, qc_ref, qp_ref, k_ref, v_ref, pos_ref, ctx_ref, p_ref,
    table_ref,
    out_ref, grad_ref, unit_ref, vec_ref,
    do_ref, dot_ref, ht_ref, dqkv_ref, dvt_ref, dkt_ref, dpt_ref,
):
    step = pl.program_id(0)
    length, features = x_ref.shape
    count = length // ROWS
    window = length + ROWS
    scale = 1.0 / math.sqrt(HEAD_DIM)

    @pl.when(step == 0)
    def _():
        vec_ref[...] = jnp.zeros(vec_ref.shape, F32)

        @pl.loop(0, count)
        def _(i):
            rows = chunk(i)
            upstream = up_ref[rows, :]
            do_ref[rows, :] = upstream.astype(BF)
            dot_ref[:, rows] = upstream.T.astype(BF)
            ht_ref[:, rows] = h_ref[rows, :].astype(F32).T.astype(BF)
            out_ref[rows, :] = jnp.zeros((ROWS, features), F32)

    dvt_ref[...] = jnp.zeros(dvt_ref.shape, F32)
    dkt_ref[...] = jnp.zeros(dkt_ref.shape, F32)
    dpt_ref[...] = jnp.zeros(dpt_ref.shape, F32)
    unit_ref[...] = jnp.zeros(unit_ref.shape, F32)

    lane = lax.broadcasted_iota(jnp.int32, (ROWS, LANES), 1) < HEAD_DIM
    mirror = (
        lax.broadcasted_iota(jnp.int32, (ROWS, ROWS), 0)
        + lax.broadcasted_iota(jnp.int32, (ROWS, ROWS), 1)
        == ROWS - 1
    ).astype(BF)
    blank = jnp.zeros((ROWS, ROWS), BF)

    @pl.loop(0, count)
    def _(i):
        rows = chunk(i)
        begin = pl.multiple_of((length - ROWS) - i * ROWS, ROWS)
        span = pl.ds(begin, window)
        positions = pos_ref[span, :]
        grad_f32 = dot(do_ref[rows, :], w_ref[:, 4 * LANES :])
        grad_ctx = grad_f32.astype(BF)
        wide_ctx = grad_ctx.astype(F32)
        weighted = wide_ctx * ctx_ref[rows, :]
        grad_ctx_t = wide_ctx.T.astype(BF)
        qc_t = qc_ref[rows, :].astype(F32).T.astype(BF)
        qp_t = dot(qp_ref[rows, :].astype(F32).T.astype(BF), mirror).astype(BF)
        from_keys = []
        from_pos = []
        for head in range(2):
            own = lane if head == 0 else jnp.logical_not(lane)
            part = slice(head * HEAD_DIM, (head + 1) * HEAD_DIM)
            center = jnp.sum(jnp.where(own, weighted, 0.0), axis=1, keepdims=True)
            grad_probs = dot(jnp.where(own, grad_ctx, jnp.zeros((), BF)), v_ref[...], NT)
            probs = p_ref[head, rows, :]
            grad_scores = (probs.astype(F32) * (grad_probs - center)).astype(BF)
            dvt_ref[part, :] += dot(grad_ctx_t[part, :], probs)
            dkt_ref[part, :] += dot(qc_t[part, :], grad_scores)
            from_keys.append(dot(grad_scores, k_ref[...]))
            flipped = dot(mirror, grad_scores).astype(BF)
            spread = pltpu.roll(
                jnp.concatenate([flipped, blank], axis=1), 0, 1, stride=1, stride_axis=0
            )
            dpt_ref[part, span] += dot(qp_t[part, :], spread)
            from_pos.append(dot(spread, positions))
        grad_c = jnp.where(lane, from_keys[0], from_keys[1]) * scale
        turned = (jnp.where(lane, from_pos[0], from_pos[1]) * scale).astype(BF)
        grad_p = dot(mirror, turned)
        dqkv_ref[rows, :LANES] = (grad_c + grad_p).astype(BF)
        unit_ref[1:2, :] += column_sum(grad_c)
        unit_ref[2:3, :] += column_sum(grad_p)

    @pl.loop(0, count)
    def _(i):
        rows = chunk(i)
        dqkv_ref[rows, LANES : 2 * LANES] = dkt_ref[:, rows].T.astype(BF)
        grad_value = dvt_ref[:, rows].T.astype(BF)
        dqkv_ref[rows, 2 * LANES :] = grad_value
        unit_ref[0:1, :] += column_sum(grad_value.astype(F32))
        out_ref[rows, :] += dot(dqkv_ref[rows, :], w_ref[:, : 3 * LANES], NT)

    @pl.loop(0, features // LANES)
    def _(i):
        rows = chunk(i, LANES)
        grad_ref[rows, : 3 * LANES] = dot(ht_ref[rows, :], dqkv_ref[...]).astype(BF)
        grad_ref[rows, 4 * LANES :] = dot(dot_ref[rows, :], ctx_ref[...].astype(BF)).astype(BF)

    grad_pos = dot(dpt_ref[...].astype(BF), table_ref[...])
    grad_ref[:, 3 * LANES : 4 * LANES] = grad_pos.T.astype(BF)

    @pl.when(step == pl.num_programs(0) - 1)
    def _():
        @pl.loop(0, count)
        def _(i):
            rows = chunk(i)
            grad_normed = out_ref[rows, :]
            normal, inverse = normal_rows(x_ref[rows, :])
            vec_ref[0:1, :] += column_sum(grad_normed * normal)
            vec_ref[1:2, :] += column_sum(grad_normed)
            out_ref[rows, :] = up_ref[rows, :] + normal_rows_back(
                grad_normed, normal, inverse, gain_ref[1:2, :]
            )


def attention_backward(upstream, x, saved, gains, weights, table, grads):
    normed, qc, qp, keys, values, pos, context, probs = saved
    length, features = x.shape
    blocks = weights.shape[0] // features
    column = pl.BlockSpec((length, LANES), lambda n: (0, n))

    def kernel(*refs):
        attention_backward_kernel(*refs[:13], *refs[14:])

    return pl.pallas_call(
        kernel,
        name="attention_backward",
        grid=(blocks,),
        in_specs=[
            full(upstream.shape),
            full(x.shape),
            full(normed.shape),
            full(gains.shape),
            pl.BlockSpec((features, 5 * LANES), lambda n: (n, 4)),
            column,
            column,
            column,
            column,
            pl.BlockSpec((2 * length, LANES), lambda n: (0, n)),
            column,
            pl.BlockSpec((2, length, length), lambda n: (n, 0, 0)),
            full(table.shape),
            pl.BlockSpec(memory_space=pl.ANY),
        ],
        out_specs=[
            full((length, features)),
            pl.BlockSpec((features, 5 * LANES), lambda n: (n, 4)),
            pl.BlockSpec((8, LANES), lambda n: (0, n)),
            full((8, features)),
        ],
        out_shape=[
            jax.ShapeDtypeStruct((length, features), F32),
            jax.ShapeDtypeStruct(grads.shape, BF),
            jax.ShapeDtypeStruct((8, features), F32),
            jax.ShapeDtypeStruct((8, features), F32),
        ],
        scratch_shapes=[
            pltpu.VMEM((length, features), BF),
            pltpu.VMEM((features, length), BF),
            pltpu.VMEM((features, length), BF),
            pltpu.VMEM((length, 3 * LANES), BF),
            pltpu.VMEM((LANES, length), F32),
            pltpu.VMEM((LANES, length), F32),
            pltpu.VMEM((LANES, 2 * length), F32),
        ],
        input_output_aliases={13: 1},
        compiler_params=params(),
    )(upstream, x, normed, gains, weights, qc, qp, keys, values, pos, context, probs, table, grads)


def tap_selector(tap_count, features, wide_count, transposed):
    shape = (features, tap_count) if transposed else (tap_count, features)
    row = lax.broadcasted_iota(jnp.int32, shape, 0 if transposed else 1)
    tap = lax.broadcasted_iota(jnp.int32, shape, 1 if transposed else 0)
    per = tap_count // wide_count
    place = tap // per * (features // wide_count) + lax.rem(tap, per)
    return (row == place).astype(BF)


def valid_rows(begin, rows, length_here):
    index = lax.broadcasted_iota(jnp.int32, (rows, 1), 0) + begin
    return (index < length_here).astype(F32)


def conv_forward_kernel(
    taps, wide_count, len_ref, x_ref, gain_ref, bias_ref, w_ref, unit_ref,
    h_ref, z_ref, mixed_ref, stat_ref,
    pad_ref, tap_ref,
):
    step = pl.program_id(0)
    length, features = x_ref.shape
    count = length // ROWS
    half = taps // 2
    valid = len_ref[0]

    @pl.when(step == 0)
    def _():
        @pl.loop(0, count)
        def _(i):
            rows = chunk(i)
            normal, _ = normal_rows(x_ref[rows, :])
            h_ref[rows, :] = (normal * gain_ref[2:3, :] + bias_ref[2:3, :]).astype(BF)
        pad_ref[:half, :] = jnp.zeros((half, LANES), F32)
        pad_ref[half + length :, :] = jnp.zeros((half, LANES), F32)

    tap_ref[...] = dot(tap_selector(taps, features, wide_count, False), w_ref[:, 3 * LANES :])

    @pl.loop(0, count)
    def _(i):
        rows = chunk(i)
        z = dot(h_ref[rows, :], w_ref[:, : 2 * LANES])
        value = z[:, :LANES] + unit_ref[3:4, :]
        gate = z[:, LANES:] + unit_ref[4:5, :]
        z_ref[rows, :LANES] = value.astype(BF)
        z_ref[rows, LANES:] = gate.astype(BF)
        glu = value * sigmoid(gate) * valid_rows(i * ROWS, ROWS, valid)
        pad_ref[pl.ds(pl.multiple_of(i * ROWS + half, 8), ROWS), :] = glu

    stat_ref[...] = jnp.zeros(stat_ref.shape, F32)

    @pl.loop(0, length // CONV_ROWS)
    def _(i):
        rows = chunk(i, CONV_ROWS)
        area = pad_ref[pl.ds(pl.multiple_of(i * CONV_ROWS, CONV_ROWS), CONV_ROWS + taps), :]
        total = jnp.zeros((CONV_ROWS, LANES), F32)
        for shift in range(8):
            moved = area[shift : shift + CONV_ROWS + taps - 8, :]
            for group in range(taps // 8):
                tap = 8 * group + shift - 1
                if tap >= 0:
                    total += tap_ref[tap : tap + 1, :] * moved[8 * group : 8 * group + CONV_ROWS, :]
        total += tap_ref[taps - 1 : taps, :] * area[taps : taps + CONV_ROWS, :]
        mixed_ref[rows, :] = total
        mask = valid_rows(i * CONV_ROWS, CONV_ROWS, valid)
        stat_ref[0:1, :] += column_sum(total * mask)

    mean = stat_ref[0:1, :] / valid.astype(F32)
    stat_ref[0:1, :] = mean

    @pl.loop(0, count)
    def _(i):
        rows = chunk(i)
        center = mixed_ref[rows, :] - mean
        stat_ref[1:2, :] += column_sum(center * center * valid_rows(i * ROWS, ROWS, valid))


def conv_forward(taps, wide_count, valid, x, gains, biases, weights, units):
    length, features = x.shape
    blocks = weights.shape[0] // features
    return pl.pallas_call(
        partial(conv_forward_kernel, taps, wide_count),
        name="conv_forward",
        grid=(blocks,),
        in_specs=[
            pl.BlockSpec(memory_space=pltpu.SMEM),
            full(x.shape),
            full(gains.shape),
            full(biases.shape),
            pl.BlockSpec((features, 4 * LANES), lambda n: (n, 4)),
            pl.BlockSpec((5, LANES), lambda n: (0, n)),
        ],
        out_specs=[
            full((length, features)),
            pl.BlockSpec((length, 2 * LANES), lambda n: (0, n)),
            pl.BlockSpec((length, LANES), lambda n: (0, n)),
            pl.BlockSpec((8, LANES), lambda n: (0, n)),
        ],
        out_shape=[
            jax.ShapeDtypeStruct((length, features), BF),
            jax.ShapeDtypeStruct((length, 2 * features), BF),
            jax.ShapeDtypeStruct((length, features), F32),
            jax.ShapeDtypeStruct((8, features), F32),
        ],
        scratch_shapes=[
            pltpu.VMEM((length + taps, LANES), F32),
            pltpu.VMEM((taps, LANES), F32),
        ],
        compiler_params=params(),
    )(valid, x, gains, biases, weights, units)


def conv_backward_kernel(
    taps, wide_count,
    len_ref, up_ref, x_ref, h_ref, gain_ref, w_ref, z_ref, mixed_ref, dbn_ref, stat_ref, affine_ref,
    out_grad_ref,
    out_ref, grad_ref, unit_ref, vec_ref,
    glu_ref, dmix_ref, tap_ref, dz_ref, ht_ref, acc_ref,
):
    step = pl.program_id(0)
    length, features = x_ref.shape
    count = length // ROWS
    half = taps // 2
    valid = len_ref[0]

    @pl.when(step == 0)
    def _():
        vec_ref[...] = jnp.zeros(vec_ref.shape, F32)

        @pl.loop(0, count)
        def _(i):
            rows = chunk(i)
            ht_ref[:, rows] = h_ref[rows, :].astype(F32).T.astype(BF)
            out_ref[rows, :] = jnp.zeros((ROWS, features), F32)
        blank = jnp.zeros((half, LANES), F32)
        glu_ref[:half, :] = blank
        glu_ref[half + length :, :] = blank
        dmix_ref[:half, :] = blank
        dmix_ref[half + length :, :] = blank

    tap_ref[...] = dot(tap_selector(taps, features, wide_count, False), w_ref[:, 3 * LANES :])

    mean = stat_ref[0:1, :]
    inverse = stat_ref[1:2, :]
    plain = stat_ref[2:3, :]
    cross = stat_ref[3:4, :]
    factor = inverse * affine_ref[0:1, :]

    @pl.loop(0, count)
    def _(i):
        rows = chunk(i)
        mask = valid_rows(i * ROWS, ROWS, valid)
        normal = (mixed_ref[rows, :] - mean) * inverse
        place = pl.ds(pl.multiple_of(i * ROWS + half, 8), ROWS)
        dmix_ref[place, :] = factor * (dbn_ref[rows, :] - mask * (plain + normal * cross))
        value = z_ref[rows, :LANES].astype(F32)
        gate = z_ref[rows, LANES:].astype(F32)
        glu_ref[place, :] = value * sigmoid(gate) * mask

    acc_ref[...] = jnp.zeros(acc_ref.shape, F32)
    unit_ref[...] = jnp.zeros(unit_ref.shape, F32)

    @pl.loop(0, length // CONV_ROWS)
    def _(i):
        rows = chunk(i, CONV_ROWS)
        around = pl.ds(pl.multiple_of(i * CONV_ROWS, CONV_ROWS), CONV_ROWS + taps)
        d_area = dmix_ref[around, :]
        g_area = glu_ref[around, :]
        here = d_area[half : half + CONV_ROWS, :]
        total = jnp.zeros((CONV_ROWS, LANES), F32)
        for shift in range(8):
            d_moved = d_area[shift : shift + CONV_ROWS + taps - 8, :]
            g_moved = g_area[shift : shift + CONV_ROWS + taps - 8, :]
            for group in range(taps // 8):
                offset = 8 * group + shift
                part = slice(8 * group, 8 * group + CONV_ROWS)
                tap = taps - 1 - offset
                total += tap_ref[tap : tap + 1, :] * d_moved[part, :]
                if offset >= 1:
                    product = (here * g_moved[part, :]).reshape(CONV_ROWS // 8, 8, LANES)
                    acc_ref[offset - 1] += jnp.sum(product, axis=0)
        product = (here * g_area[taps : taps + CONV_ROWS, :]).reshape(CONV_ROWS // 8, 8, LANES)
        acc_ref[taps - 1] += jnp.sum(product, axis=0)
        grad_glu = total * valid_rows(i * CONV_ROWS, CONV_ROWS, valid)
        value = z_ref[rows, :LANES].astype(F32)
        sigma = sigmoid(z_ref[rows, LANES:].astype(F32))
        grad_value = (grad_glu * sigma).astype(BF)
        grad_gate = (grad_glu * value * sigma * (1.0 - sigma)).astype(BF)
        dz_ref[rows, :LANES] = grad_value
        dz_ref[rows, LANES:] = grad_gate
        unit_ref[0:1, :] += column_sum(grad_value.astype(F32))
        unit_ref[1:2, :] += column_sum(grad_gate.astype(F32))

    @pl.loop(0, count)
    def _(i):
        rows = chunk(i)
        out_ref[rows, :] += dot(dz_ref[rows, :], w_ref[:, : 2 * LANES], NT)

    grad_ref[:, : 2 * LANES] = dot(ht_ref[...], dz_ref[...]).astype(BF)
    grad_ref[:, 2 * LANES : 3 * LANES] = out_grad_ref[...]
    grad_taps = jnp.sum(acc_ref[...], axis=1)
    grad_ref[:, 3 * LANES :] = dot(
        tap_selector(taps, features, wide_count, True), grad_taps.astype(BF)
    ).astype(BF)

    @pl.when(step == pl.num_programs(0) - 1)
    def _():
        @pl.loop(0, count)
        def _(i):
            rows = chunk(i)
            grad_normed = out_ref[rows, :]
            normal, inverse_row = normal_rows(x_ref[rows, :])
            vec_ref[0:1, :] += column_sum(grad_normed * normal)
            vec_ref[1:2, :] += column_sum(grad_normed)
            result = up_ref[rows, :] + normal_rows_back(
                grad_normed, normal, inverse_row, gain_ref[2:3, :]
            )
            vec_ref[2:3, :] += column_sum(result)
            out_ref[rows, :] = result


def conv_backward(
    taps, wide_count, valid, upstream, x, h, gains, weights, z, mixed, dbn, stats, affine,
    out_grad, grads,
):
    length, features = x.shape
    blocks = weights.shape[0] // features
    column = pl.BlockSpec((length, LANES), lambda n: (0, n))

    def kernel(*refs):
        conv_backward_kernel(taps, wide_count, *refs[:12], *refs[13:])

    return pl.pallas_call(
        kernel,
        name="conv_backward",
        grid=(blocks,),
        in_specs=[
            pl.BlockSpec(memory_space=pltpu.SMEM),
            full(upstream.shape),
            full(x.shape),
            full(h.shape),
            full(gains.shape),
            pl.BlockSpec((features, 4 * LANES), lambda n: (n, 4)),
            pl.BlockSpec((length, 2 * LANES), lambda n: (0, n)),
            column,
            column,
            pl.BlockSpec((8, LANES), lambda n: (0, n)),
            pl.BlockSpec((2, LANES), lambda n: (0, n)),
            pl.BlockSpec((features, LANES), lambda n: (n, 0)),
            pl.BlockSpec(memory_space=pl.ANY),
        ],
        out_specs=[
            full((length, features)),
            pl.BlockSpec((features, 4 * LANES), lambda n: (n, 4)),
            pl.BlockSpec((8, LANES), lambda n: (0, n)),
            full((8, features)),
        ],
        out_shape=[
            jax.ShapeDtypeStruct((length, features), F32),
            jax.ShapeDtypeStruct(grads.shape, BF),
            jax.ShapeDtypeStruct((8, features), F32),
            jax.ShapeDtypeStruct((8, features), F32),
        ],
        scratch_shapes=[
            pltpu.VMEM((length + taps, LANES), F32),
            pltpu.VMEM((length + taps, LANES), F32),
            pltpu.VMEM((taps, LANES), F32),
            pltpu.VMEM((length, 2 * LANES), BF),
            pltpu.VMEM((features, length), BF),
            pltpu.VMEM((taps, 8, LANES), F32),
        ],
        input_output_aliases={12: 1},
        compiler_params=params(),
    )(valid, upstream, x, h, gains, weights, z, mixed, dbn, stats, affine, out_grad, grads)


def middle_kernel(
    len_ref, x2_ref, cot_ref, gain_ref, bias_ref, mixed_ref, stat_ref, affine_ref, wc_ref, wf_ref,
    hidden_ref,
    final_ref, dx3_ref, grad_ref, hidden_grad_ref, vec_ref, dbn_ref, sums_ref, out_grad_ref,
    x3_ref, dx4_ref, h_ref, ht_ref, df_ref, dft_ref, a_ref, s_ref, da_ref,
):
    phase = pl.program_id(0)
    step = pl.program_id(1)
    last = pl.num_programs(1) - 1
    length, features = x2_ref.shape
    count = length // ROWS
    width = hidden_ref.shape[1]
    valid = len_ref[0]
    mean = stat_ref[0:1, :]
    inverse_bn = stat_ref[1:2, :]

    @pl.when(phase == 0)
    def _():
        @pl.when(step == 0)
        def _():
            vec_ref[...] = jnp.zeros(vec_ref.shape, F32)

            @pl.loop(0, count)
            def _(i):
                rows = chunk(i)
                x3_ref[rows, :] = x2_ref[rows, :] + bias_ref[7:8, :]

        @pl.loop(0, count)
        def _(i):
            rows = chunk(i)
            normal = (mixed_ref[rows, :] - mean) * inverse_bn
            bn = normal * affine_ref[0:1, :] + affine_ref[1:2, :]
            act = (bn * sigmoid(bn)).astype(BF)
            x3_ref[rows, :] += dot(act, wc_ref[:, 2 * LANES : 3 * LANES], NT)

        @pl.when(step == last)
        def _():
            @pl.loop(0, count)
            def _(i):
                rows = chunk(i)
                normal, _ = normal_rows(x3_ref[rows, :])
                hidden = normal * gain_ref[3:4, :] + bias_ref[3:4, :]
                h_ref[rows, :] = hidden.astype(BF)
                ht_ref[:, rows] = hidden.T.astype(BF)
                dx4_ref[rows, :] = jnp.zeros((ROWS, features), F32)

    @pl.when(phase == 1)
    def _():
        @pl.loop(0, count)
        def _(i):
            rows = chunk(i)
            pre = dot(h_ref[rows, :], wf_ref[:, :width]) + hidden_ref[1:2, :]
            a_ref[step, rows, :] = pre
            act = (pre * sigmoid(pre)).astype(BF)
            dx4_ref[rows, :] += dot(act, wf_ref[:, width:], NT)

        @pl.when(step == last)
        def _():
            @pl.loop(0, count)
            def _(i):
                rows = chunk(i)
                x4 = x3_ref[rows, :] + 0.5 * (dx4_ref[rows, :] + bias_ref[8:9, :])
                normal, inverse = normal_rows(x4)
                final_ref[rows, :] = (normal * gain_ref[4:5, :] + bias_ref[4:5, :]).astype(BF)
                upstream = cot_ref[rows, :].astype(F32) * valid_rows(i * ROWS, ROWS, valid)
                vec_ref[0:1, :] += column_sum(upstream * normal)
                vec_ref[1:2, :] += column_sum(upstream)
                dx4 = normal_rows_back(upstream, normal, inverse, gain_ref[4:5, :])
                dx4_ref[rows, :] = dx4
                half = 0.5 * dx4
                vec_ref[2:3, :] += column_sum(half)
                df_ref[rows, :] = half.astype(BF)
                dft_ref[:, rows] = half.T.astype(BF)
                dx3_ref[rows, :] = jnp.zeros((ROWS, features), F32)

    @pl.when(phase == 2)
    def _():
        hidden_grad_ref[...] = jnp.zeros(hidden_grad_ref.shape, F32)

        @pl.loop(0, count)
        def _(i):
            rows = chunk(i)
            pre = a_ref[step, rows, :]
            sigma = sigmoid(pre)
            s_ref[rows, :] = (pre * sigma).astype(BF)
            grad_act = dot(df_ref[rows, :], wf_ref[:, width:])
            grad_pre = (grad_act * (sigma * (1.0 + pre * (1.0 - sigma)))).astype(BF)
            da_ref[rows, :] = grad_pre
            hidden_grad_ref[...] += column_sum(grad_pre.astype(F32))
            dx3_ref[rows, :] += dot(grad_pre, wf_ref[:, :width], NT)

        @pl.loop(0, features // LANES)
        def _(i):
            rows = chunk(i, LANES)
            grad_ref[rows, :width] = dot(ht_ref[rows, :], da_ref[...]).astype(BF)
            grad_ref[rows, width:] = dot(dft_ref[rows, :], s_ref[...]).astype(BF)

        @pl.when(step == last)
        def _():
            @pl.loop(0, count)
            def _(i):
                rows = chunk(i)
                grad_normed = dx3_ref[rows, :]
                normal, inverse = normal_rows(x3_ref[rows, :])
                vec_ref[3:4, :] += column_sum(grad_normed * normal)
                vec_ref[4:5, :] += column_sum(grad_normed)
                result = dx4_ref[rows, :] + normal_rows_back(
                    grad_normed, normal, inverse, gain_ref[3:4, :]
                )
                vec_ref[5:6, :] += column_sum(result)
                dx3_ref[rows, :] = result
                df_ref[rows, :] = result.astype(BF)
                dft_ref[:, rows] = result.T.astype(BF)

    @pl.when(phase == 3)
    def _():
        sums_ref[...] = jnp.zeros(sums_ref.shape, F32)

        @pl.loop(0, count)
        def _(i):
            rows = chunk(i)
            normal = (mixed_ref[rows, :] - mean) * inverse_bn
            bn = normal * affine_ref[0:1, :] + affine_ref[1:2, :]
            sigma = sigmoid(bn)
            s_ref[rows, :LANES] = (bn * sigma).astype(BF)
            grad_act = dot(df_ref[rows, :], wc_ref[:, 2 * LANES : 3 * LANES])
            grad_bn = grad_act * (sigma * (1.0 + bn * (1.0 - sigma)))
            dbn_ref[rows, :] = grad_bn
            sums_ref[0:1, :] += column_sum(grad_bn)
            sums_ref[1:2, :] += column_sum(grad_bn * normal)

        out_grad_ref[...] = dot(dft_ref[...], s_ref[:, :LANES]).astype(BF)


def middle(valid, x2, cotangent, gains, biases, mixed, stats, affine, weights, hidden):
    length, features = x2.shape
    blocks = weights.shape[0] // features
    width = hidden.shape[1] // blocks
    final = blocks - 1

    def outer(phase, n):
        return jnp.where((phase == 0) | (phase == 3), n, final)

    def late(phase, n):
        return jnp.where(phase == 3, n, 0)

    def inner(phase, n):
        return jnp.where(phase == 0, 0, jnp.where(phase == 3, final, n))

    def backs(phase, n):
        return jnp.where(phase < 2, 0, jnp.where(phase == 3, final, n))

    return pl.pallas_call(
        middle_kernel,
        name="middle",
        grid=(4, blocks),
        in_specs=[
            pl.BlockSpec(memory_space=pltpu.SMEM),
            full(x2.shape),
            full(cotangent.shape),
            full(gains.shape),
            full(biases.shape),
            pl.BlockSpec((length, LANES), lambda p, n: (0, outer(p, n))),
            pl.BlockSpec((8, LANES), lambda p, n: (0, outer(p, n))),
            pl.BlockSpec((2, LANES), lambda p, n: (0, outer(p, n))),
            pl.BlockSpec((features, 4 * LANES), lambda p, n: (outer(p, n), 4)),
            pl.BlockSpec((features, 2 * width), lambda p, n: (inner(p, n), 1)),
            pl.BlockSpec((2, width), lambda p, n: (0, inner(p, n))),
        ],
        out_specs=[
            full((length, features)),
            full((length, features)),
            pl.BlockSpec((features, 2 * width), lambda p, n: (backs(p, n), 1)),
            pl.BlockSpec((1, width), lambda p, n: (0, backs(p, n))),
            full((8, features)),
            pl.BlockSpec((length, LANES), lambda p, n: (0, late(p, n))),
            pl.BlockSpec((8, LANES), lambda p, n: (0, late(p, n))),
            pl.BlockSpec((features, LANES), lambda p, n: (late(p, n), 0)),
        ],
        out_shape=[
            jax.ShapeDtypeStruct((length, features), BF),
            jax.ShapeDtypeStruct((length, features), F32),
            jax.ShapeDtypeStruct(weights.shape, BF),
            jax.ShapeDtypeStruct((1, blocks * width), F32),
            jax.ShapeDtypeStruct((8, features), F32),
            jax.ShapeDtypeStruct((length, features), F32),
            jax.ShapeDtypeStruct((8, features), F32),
            jax.ShapeDtypeStruct((blocks * features, LANES), BF),
        ],
        scratch_shapes=[
            pltpu.VMEM((length, features), F32),
            pltpu.VMEM((length, features), F32),
            pltpu.VMEM((length, features), BF),
            pltpu.VMEM((features, length), BF),
            pltpu.VMEM((length, features), BF),
            pltpu.VMEM((features, length), BF),
            pltpu.VMEM((blocks, length, width), F32),
            pltpu.VMEM((length, width), BF),
            pltpu.VMEM((length, width), BF),
        ],
        compiler_params=params(),
    )(valid, x2, cotangent, gains, biases, mixed, stats, affine, weights, weights, hidden)


def position_table(length, feature_count):
    step = 32
    column = np.arange(feature_count)
    frequency = np.exp((column // 2) * (-2.0 * math.log(10000.0) / feature_count))
    phase = (column % 2) * (math.pi / 2)
    high = (length - 1 - step * np.arange(2 * length // step))[:, None] * frequency[None, :]
    low = -np.arange(step)[:, None] * frequency[None, :] + phase[None, :]
    high_sin, high_cos, low_sin, low_cos = (
        jnp.asarray(part.astype(np.float32))
        for part in (np.sin(high), np.cos(high), np.sin(low), np.cos(low))
    )
    table = high_sin[:, None, :] * low_cos[None] + high_cos[:, None, :] * low_sin[None]
    return table.reshape(2 * length, feature_count).astype(BF)


def shards(
    mesh_shape,
    inputs,
    cotangent,
    lengths,
    ffn1_in,
    ffn1_out,
    attn_in,
    pos_proj,
    attn_out,
    conv_in,
    depthwise,
    conv_out,
    ffn2_in,
    ffn2_out,
    row_gains,
    row_biases,
    unit_biases,
    ffn_biases,
    norm_affine,
):
    narrow, wide = mesh_shape["narrow"], mesh_shape["wide"]
    both = ("narrow", "wide")
    micros, frames, utters, features = inputs.shape
    streams = micros * utters
    copies = narrow // streams
    assert copies * streams == narrow
    length = frames * narrow
    blocks = features // LANES
    depth = features // wide
    each = attn_out.shape[0]
    hidden_each = ffn_biases.shape[1]
    taps_each = depthwise.shape[0]
    taps = taps_each * wide
    narrow_index = lax.axis_index("narrow")
    stream_index = narrow_index // copies

    smalls = jnp.concatenate(
        [unit_biases, norm_affine, ffn_biases.reshape(-1, each)], axis=0
    )
    extra = jnp.concatenate([depthwise, smalls], axis=0)
    extra = jnp.pad(extra, ((0, depth - extra.shape[0]), (0, 0)))
    packed = jnp.concatenate(
        [
            ffn1_in,
            ffn1_out.T,
            ffn2_in,
            ffn2_out.T,
            conv_in.reshape(depth, -1),
            conv_out.T,
            extra,
            attn_in.reshape(depth, -1),
            pos_proj,
            attn_out.T,
        ],
        axis=1,
    )
    kinds = (
        (1, hidden_each), (1, hidden_each), (1, hidden_each), (1, hidden_each),
        (2, each), (1, each), (1, each), (3, each), (1, each), (1, each),
    )
    gathered = lax.all_gather(packed, both, axis=0, tiled=True)

    def pieces(array, parts_of):
        begin = 0
        for many, size in parts_of:
            yield array[..., begin : begin + many * size], many, size
            begin += many * size

    small_rows = gathered.reshape(narrow, features, -1)[
        :, taps_each : taps_each + SMALL_ROWS, 4 * hidden_each + 3 * each : 4 * hidden_each + 4 * each
    ].astype(F32)
    units = jnp.moveaxis(small_rows[:, :5], 0, 1).reshape(5, features)
    affine = jnp.moveaxis(small_rows[:, 5:7], 0, 1).reshape(2, features)
    hidden_biases = jnp.moveaxis(
        small_rows[:, 7:].reshape(narrow, 2, hidden_each), 0, 1
    ).reshape(2, -1)
    if narrow != blocks:
        regrouped = []
        for part, many, size in pieces(gathered.reshape(narrow, features, -1), kinds):
            part = part.reshape(narrow, features, many, size)
            part = part.transpose(1, 2, 0, 3).reshape(features, many, blocks, -1)
            regrouped.append(part.transpose(2, 0, 1, 3).reshape(blocks * features, -1))
        gathered = jnp.concatenate(regrouped, axis=1)

    gains = row_gains.astype(F32)
    biases = row_biases.astype(F32)
    table = position_table(length, features)

    def to_stream(array):
        moved = array.transpose(0, 2, 1, 3).reshape(streams, frames, features)
        if copies > 1:
            moved = jnp.repeat(moved, copies, axis=0)
        moved = lax.all_to_all(moved, "narrow", 0, 0, tiled=True)
        return moved.reshape(length, features)

    def from_stream(array):
        moved = lax.all_to_all(
            array.reshape(narrow, frames, features), "narrow", 0, 0, tiled=True
        )[::copies]
        return moved.reshape(micros, utters, frames, features).transpose(0, 2, 1, 3)

    x0 = to_stream(inputs)
    upstream = to_stream(cotangent)
    valid = lax.dynamic_slice(lengths.reshape(-1), (stream_index,), (1,))
    masked = jnp.where(jnp.arange(length)[None, :] < valid, 0.0, MASKED).astype(F32)

    hops = [("narrow", copies << bit) for bit in range(utters.bit_length() - 1)]
    hops += [("wide", 1 << bit) for bit in range(wide.bit_length() - 1)]

    def swap(array, axis, mask):
        size = mesh_shape[axis]
        return lax.ppermute(array, axis, [(i, i ^ mask) for i in range(size)])

    def merge_moments(local_stats, local_valid):
        size = jnp.broadcast_to(local_valid.astype(F32), (1, features))
        state = jnp.concatenate([local_stats[:2], size], axis=0)
        for axis, mask in hops:
            other = swap(state, axis, mask)
            total = state[2:] + other[2:]
            delta = other[:1] - state[:1]
            share = other[2:] / total
            state = jnp.concatenate(
                [
                    state[:1] + delta * share,
                    state[1:2] + other[1:2] + delta * delta * state[2:] * share,
                    total,
                ],
                axis=0,
            )
        return state

    def merge_sums(state):
        for axis, mask in hops:
            state = state + swap(state, axis, mask)
        return state

    x1, a_first = ffn_forward(x0, gains, biases, gathered, hidden_biases)
    x2, *saved = attention_forward(x1, gains, biases, gathered, units, table, masked)
    h3, z, mixed, local_stats = conv_forward(
        taps, wide, valid, x2, gains, biases, gathered, units
    )
    moments = merge_moments(local_stats, valid)
    number = moments[2:]
    stats = jnp.concatenate([moments[:1], lax.rsqrt(moments[1:2] / number + EPSILON)], axis=0)
    stats = jnp.pad(stats, ((0, 6), (0, 0)))

    final, dx3, grads, hidden_second, vec_mid, dbn, local_sums, out_grad = middle(
        valid, x2, upstream, gains, biases, mixed, stats, affine, gathered, hidden_biases
    )
    sums = merge_sums(local_sums[:2])
    stats = jnp.concatenate([stats[:2], sums / number, jnp.zeros((4, features), F32)], axis=0)
    dx2, grads, unit_conv, vec_conv = conv_backward(
        taps, wide, valid, dx3, x2, h3, gains, gathered, z, mixed, dbn, stats, affine,
        out_grad, grads,
    )
    dx1, grads, unit_att, vec_att = attention_backward(
        dx2, x1, saved, gains, gathered, table, grads
    )
    dx0, grads, hidden_first, vec_first = ffn_backward(
        dx1, x0, gains, biases, gathered, a_first, grads
    )

    layer_out = from_stream(final)
    input_grad = from_stream(dx0.astype(BF)).astype(F32)

    vectors = jnp.concatenate(
        [
            vec_first[0:1], vec_att[0:1], vec_conv[0:1], vec_mid[3:4], vec_mid[0:1],
            vec_first[1:2], vec_att[1:2], vec_conv[1:2], vec_mid[4:5], vec_mid[1:2],
            vec_first[2:3], vec_conv[2:3], vec_mid[5:6], vec_mid[2:3],
            unit_att[:3], unit_conv[:2],
            local_sums[1:2], local_sums[0:1],
            hidden_first.reshape(-1, features), hidden_second.reshape(-1, features),
        ],
        axis=0,
    )
    vectors = lax.psum(vectors, both) * (1.0 / copies)
    grad_gains = vectors[:5]
    grad_biases = vectors[5:14]

    def own_columns(array, size):
        return lax.dynamic_slice_in_dim(array, narrow_index * size, size, 1)

    grad_units = own_columns(vectors[14:19], each)
    grad_affine = own_columns(vectors[19:21], each)
    grad_hidden = own_columns(vectors[21:].reshape(2, -1), hidden_each)

    if narrow != blocks:
        ratio = narrow // blocks
        regrouped = []
        block_kinds = tuple((many, size * ratio) for many, size in kinds)
        for part, many, size in pieces(grads.reshape(blocks, features, -1), block_kinds):
            part = part.reshape(blocks, features, many, ratio, size // ratio)
            part = part.transpose(0, 3, 1, 2, 4)
            regrouped.append(part.reshape(narrow * features, -1))
        grads = jnp.concatenate(regrouped, axis=1)
    reduced = lax.psum_scatter(grads, both, scatter_dimension=0, tiled=True)
    if copies > 1:
        reduced = reduced * (1.0 / copies)
    outs = [part.astype(F32) for part, _, _ in pieces(reduced, kinds)]
    return (
        layer_out,
        input_grad,
        outs[0],
        outs[1].T,
        outs[7].reshape(depth, 3, each),
        outs[8],
        outs[9].T,
        outs[4].reshape(depth, 2, each),
        outs[6][:taps_each],
        outs[5].T,
        outs[2],
        outs[3].T,
        grad_gains,
        grad_biases,
        grad_units,
        grad_hidden,
        grad_affine,
    )


def solution(mesh):
    shape = dict(mesh.shape)
    matrix_in = P("wide", "narrow")
    matrix_out = P("narrow", "wide")
    stacked = P("wide", None, "narrow")
    stream = P(None, "narrow", "wide", None)
    weights = (
        matrix_in, matrix_out, stacked, matrix_in, matrix_out,
        stacked, matrix_in, matrix_out, matrix_in, matrix_out,
    )
    vectors = (P(), P(), P(None, "narrow"), P(None, "narrow"), P(None, "narrow"))
    return jax.shard_map(
        partial(shards, shape),
        mesh=mesh,
        in_specs=(stream, stream, P(None, "wide")) + weights + vectors,
        out_specs=(stream, stream) + weights + vectors,
        check_vma=False,
    )
```
